512 devices in a mesh: doc: 32 (over x, y), term: 16 (over z, core).
Axes of the slice: x: 4, y: 8, z: 8, core: 2. Of those that a mesh axis runs over, the one named last changes fastest.
Arguments:
- doc_tiles: bfloat16 [4096, 24, 2048], P('doc', None, 'term'), may hold values from -8 to 8
- tile_list: int32 [32, 24], replicated, may hold values from 0 to 127, as said below
Outputs:
- cosine: float32 [4096, 4096], P(('doc', 'term'))
The draws below stay inside these ranges and needn't reach their ends.
Inputs may be any that keep to these rules, and one draw needn't show every extreme that they name: `tile_list`: each row names 24 different term blocks.
All inputs are finite; a program needn't handle non-finite values.
Results may differ from the reference program's by a relative error of at most 0.0003.
Values may be sent and summed in bfloat16 or wider, within the bound.
No kernel may reach another device: no remote copies, remote signals or barrier semaphores. Data moves between devices by JAX's collectives and lax.ppermute only.
A program may use at most 64 MiB of HBM per device.

```python
import jax
import jax.numpy as jnp
from jax import lax

ROWS = 128
TB = 2048
VOCAB = 262144
NNZ = 24
DOCS = 4096
N_TERM = 16


def term_choices(key):
    block_count = DOCS // ROWS
    block_kinds = VOCAB // TB
    favour_level = jax.random.randint(jax.random.fold_in(key, 11), (block_kinds,), 0, 4)
    jitter = jax.random.randint(jax.random.fold_in(key, 12), (block_count, block_kinds), 0, 2 ** 19)
    scores = (jitter + favour_level[None, :] * 2 ** 18) * block_kinds + jnp.arange(block_kinds, dtype=jnp.int32)[None, :]
    return lax.top_k(scores, NNZ)[1].astype(jnp.int32)


def draw_tile_list(key, part):
    return term_choices(key)


def draw_doc_tiles(key, part):
    block_count = DOCS // ROWS
    block_kinds = VOCAB // TB
    chosen = term_choices(key)
    profile = jax.random.normal(jax.random.fold_in(key, 21), (block_kinds, TB), jnp.float32)
    picked = profile[chosen]
    weights = jnp.exp(jax.random.uniform(jax.random.fold_in(key, 22), (block_count, ROWS, NNZ, 1), jnp.float32, -1.2, 0.7))
    roughness = 0.7 * jax.random.normal(jax.random.fold_in(key, 23), (block_count, ROWS, NNZ, TB), jnp.float32)
    values = weights * picked[:, None, :, :] + roughness
    return jnp.clip(values, -8.0, 8.0).reshape(DOCS, NNZ, TB).astype(jnp.bfloat16)


def setup_inputs(seed: int = 0) -> dict:
    streams_of = jax.random.split(jax.random.key(seed), 3)
    doc_tiles = draw_doc_tiles(jax.random.fold_in(streams_of[2], 71), 0)
    tile_list = draw_tile_list(jax.random.fold_in(streams_of[2], 71), 0)
    return {"doc_tiles": doc_tiles, "tile_list": tile_list}


epsilon = 1e-06

def reference(doc_tiles, tile_list):
    block_count = DOCS // ROWS
    term_width = TB // N_TERM
    blocks = doc_tiles.reshape(block_count, ROWS, NNZ, N_TERM, term_width)
    squares = lax.optimization_barrier(jnp.sum(jnp.square(doc_tiles.astype(jnp.float32)), axis=(1, 2)))
    row_norms = jnp.sqrt(squares + epsilon)

    def one_row(left_index):
        left_tiles = blocks[left_index].astype(jnp.float32)
        left_terms = tile_list[left_index]

        def one_pair(right_index):
            right_tiles = blocks[right_index].astype(jnp.float32)
            selector = (left_terms[:, None] == tile_list[right_index][None, :]).astype(jnp.float32)
            aligned = jnp.einsum('ab,sbtc->satc', selector, right_tiles)
            partial_sums = jnp.einsum('ratc,satc->trs', left_tiles, aligned)
            return lax.optimization_barrier(jnp.sum(partial_sums, axis=0))
        return lax.map(one_pair, jnp.arange(block_count, dtype=jnp.int32))
    gram_matrix = lax.map(one_row, jnp.arange(block_count, dtype=jnp.int32))
    gram_matrix = jnp.transpose(gram_matrix, (0, 2, 1, 3)).reshape(DOCS, DOCS)
    return gram_matrix / (row_norms[:, None] * row_norms[None, :])
```

```python
import functools

import jax
import jax.numpy as jnp
from jax import lax
from jax.experimental import pallas as pl
from jax.experimental.pallas import tpu as pltpu
from jax.sharding import Mesh
from jax.sharding import PartitionSpec as P


EPSILON = 1e-06
NX, NY, NZ, NC = 4, 8, 8, 2
AXES = ("x", "y", "z", "core")
SLOTS, ROWS, WIDTH = 24, 128, 128
SUB = 8
DEPTH = SLOTS * WIDTH


def send(value, dx=0, dy=0, flip=False):
    pairs = []
    for x in range(NX):
        for y in range(NY):
            for z in range(NZ):
                for c in range(NC):
                    source = ((x * NY + y) * NZ + z) * NC + c
                    target = (((x + dx) % NX * NY + (y + dy) % NY) * NZ + z) * NC + (1 - c if flip else c)
                    pairs.append((source, target))
    return lax.ppermute(value, AXES, pairs)


def gram_kernel(offsets, pieces, n_squares, meta, table, *refs):
    left = refs[:NX]
    right = refs[NX : NX + sum(pieces)]
    squares_in = refs[NX + sum(pieces) : NX + sum(pieces) + n_squares]
    mine, theirs, squares_out, aligned, product = refs[NX + sum(pieces) + n_squares :]
    x, core = meta[0], meta[3]
    row_of = lax.broadcasted_iota(jnp.int32, (SUB, ROWS), 0)
    squares = jnp.zeros((SUB, ROWS), jnp.float32)
    for ref in squares_in:
        squares = squares + ref[...]
    first = 0
    for i, offset in enumerate(offsets):
        parts = right[first : first + pieces[i]]
        first += pieces[i]
        tiles = [part[e] for part in parts for e in range(part.shape[0])]
        for j in range(NX):
            for e in range(SLOTS):
                a = table[(offset * NX + j) * SLOTS + e]
                tile = left[j][jnp.maximum(a, 0)]
                aligned[j * ROWS : (j + 1) * ROWS, e * WIDTH : (e + 1) * WIDTH] = jnp.where(
                    a >= 0, tile, jnp.zeros_like(tile)
                )
        product[...] = lax.dot_general(
            aligned[...],
            jnp.concatenate(tiles, axis=1),
            (((1,), (1,)), ((), ())),
            preferred_element_type=jnp.float32,
        )
        total = jnp.zeros((ROWS, WIDTH), jnp.float32)
        for tile in tiles:
            wide = tile.astype(jnp.float32)
            total = total + wide * wide
        row_sums = lax.dot_general(
            jnp.ones((SUB, WIDTH), jnp.float32),
            total,
            (((1,), (1,)), ((), ())),
            preferred_element_type=jnp.float32,
            precision=lax.Precision.HIGHEST,
        )
        squares = jnp.where(row_of == offset, row_sums, squares)
        for j in range(NX):
            owner = lax.rem(x + j, NX) * NZ
            for z in range(NZ):
                base = j * ROWS + z * NC * SUB
                columns = slice(i * WIDTH, (i + 1) * WIDTH)
                mine[owner + z, :SUB, columns] = product[pl.ds(pl.multiple_of(base + core * SUB, SUB), SUB), :]
                theirs[owner + z, :SUB, columns] = product[
                    pl.ds(pl.multiple_of(base + (1 - core) * SUB, SUB), SUB), :
                ]
    squares_out[...] = squares
    if mine.shape[1] == 2 * SUB:
        for k in range(NX * NZ):
            mine[k, SUB:, :] = squares
            theirs[k, SUB:, :] = squares


def gram_part(meta, table, left, right, offsets, squares, last=False):
    pieces = [len(block) for block in right]
    flat = [piece for block in right for piece in block]
    height = 2 * SUB if last else SUB
    message = jax.ShapeDtypeStruct((NX * NZ, height, len(offsets) * WIDTH), jnp.float32)
    vmem = pl.BlockSpec(memory_space=pltpu.VMEM)
    smem = pl.BlockSpec(memory_space=pltpu.SMEM)
    count = len(offsets)
    return pl.pallas_call(
        functools.partial(gram_kernel, tuple(offsets), tuple(pieces), len(squares)),
        out_shape=(message, message, jax.ShapeDtypeStruct((SUB, ROWS), jnp.float32)),
        in_specs=[smem, smem] + [vmem] * (NX + len(flat) + len(squares)),
        out_specs=(vmem, vmem, vmem),
        scratch_shapes=[
            pltpu.VMEM((NX * ROWS, DEPTH), jnp.bfloat16),
            pltpu.VMEM((NX * ROWS, WIDTH), jnp.float32),
        ],
        cost_estimate=pl.CostEstimate(
            flops=count * 2 * NX * ROWS * WIDTH * DEPTH, bytes_accessed=(NX + count) * 786432, transcendentals=0
        ),
        compiler_params=pltpu.CompilerParams(vmem_limit_bytes=24 << 20),
        name="gram_part",
    )(meta, table, *left, *flat, *squares)


def finish_kernel(groups, meta, *refs):
    parts, out = refs[:-1], refs[-1]
    x, y, t = meta[0], meta[1], meta[2] * NC + meta[3]
    last = parts[-1]

    def summed(ref, source, rows, columns):
        total = ref[source * NZ, rows, columns]
        for z in range(1, NZ):
            total = total + ref[source * NZ + z, rows, columns]
        return total

    def norms_of(source):
        return jnp.sqrt(summed(last, source, slice(SUB, 2 * SUB), slice(0, WIDTH)) + EPSILON)

    lane = lax.broadcasted_iota(jnp.int32, (SUB, ROWS), 1)
    row = lax.broadcasted_iota(jnp.int32, (SUB, ROWS), 0)
    own = jnp.broadcast_to(norms_of(x)[:1], (SUB, ROWS))
    row_norms = jnp.sum(jnp.where(lane == t * SUB + row, own, 0.0), axis=1, keepdims=True)
    for source in range(NX):
        norms = norms_of(source)
        for ref, offsets in zip(parts, groups):
            for i, offset in enumerate(offsets):
                gram = summed(ref, source, slice(0, SUB), slice(i * WIDTH, (i + 1) * WIDTH))
                column = pl.multiple_of((source * NY + lax.rem(y + offset, NY)) * ROWS, ROWS)
                out[:, pl.ds(column, ROWS)] = gram / (row_norms * norms[offset : offset + 1])


def finish(meta, parts, groups):
    vmem = pl.BlockSpec(memory_space=pltpu.VMEM)
    return pl.pallas_call(
        functools.partial(finish_kernel, groups),
        out_shape=jax.ShapeDtypeStruct((SUB, NX * NY * ROWS), jnp.float32),
        in_specs=[pl.BlockSpec(memory_space=pltpu.SMEM)] + [vmem] * len(parts),
        out_specs=vmem,
        compiler_params=pltpu.CompilerParams(vmem_limit_bytes=8 << 20),
        name="finish",
    )(meta, *parts)


def to_owners(mine, theirs):
    both = mine + send(theirs, flip=True)
    return lax.all_to_all(both, ("x", "z"), split_axis=0, concat_axis=0, tiled=True)


def shards(doc_tiles, tile_list):
    x, y = lax.axis_index("x"), lax.axis_index("y")
    meta = jnp.stack([x, y, lax.axis_index("z"), lax.axis_index("core")]).astype(jnp.int32)
    own = jnp.transpose(doc_tiles, (1, 0, 2))

    up1, down1 = send(own, dy=-1), send(own, dy=1)
    right1, left1 = send(own, dx=-1), send(own, dx=1)
    up2, down2 = send(up1, dy=-1), send(down1, dy=1)
    half = SLOTS // 2
    right2 = send(right1, dx=-1)
    up3, down3 = send(up2, dy=-1), send(down2, dy=1)
    far = (send(up3[:half], dy=-1), send(down3[half:], dy=1))

    lists = tile_list.reshape(NX, NY, SLOTS)
    columns = jnp.roll(lax.dynamic_index_in_dim(lists, x, 0, keepdims=False), -y, axis=0)
    rows = jnp.roll(lax.dynamic_index_in_dim(lists, y, 1, keepdims=False), -x, axis=0)
    same = columns[:, None, :, None] == rows[None, :, None, :]
    slot = lax.broadcasted_iota(jnp.int32, same.shape, 3)
    table = jnp.max(jnp.where(same, slot, -1), axis=3).reshape(-1)

    blocks = (own, right1, right2, left1)
    groups = ((0, 1, 7), (2, 6, 3, 5), (4,))
    rights = (((own,), (up1,), (down1,)), ((up2,), (down2,), (up3,), (down3,)), (far,))
    squares = []
    arrived = []
    for k, (offsets, right) in enumerate(zip(groups, rights)):
        final = k == len(groups) - 1
        mine, theirs, square = gram_part(meta, table, blocks, right, offsets, squares if final else [], final)
        squares.append(square)
        arrived.append(to_owners(mine, theirs))
    return finish(meta, arrived, groups)


def solution(mesh):
    grid = Mesh(mesh.devices.reshape(NX, NY, NZ, NC), AXES)
    return jax.shard_map(
        shards,
        mesh=grid,
        in_specs=(P(("x", "y"), None, ("z", "core")), P()),
        out_specs=P(AXES, None),
        check_vma=False,
    )
```
